32 devices in a mesh: ctx: 8 (over z, x), head: 4 (over y, core).
Axes of the slice: x: 2, y: 2, z: 4, core: 2. Of those that a mesh axis runs over, the one named last changes fastest.
Arguments:
- q_latent: bfloat16 [1024, 1536], P('ctx'), may hold values from -6 to 6
- latent_bias: float32 [8, 1536], P('ctx'), may hold values from -3 to 3
- norm_gain: float32 [1536], replicated, may hold values from 0.5 to 1.5
- w_q: bfloat16 [1536, 24576], P('ctx', 'head'), may hold values from -0.15625 to 0.15625
- steer: float32 [8, 24576], P('ctx', 'head'), may hold values from -10 to 10
- kv_latent: bfloat16 [1024, 512], P('ctx'), may hold values from -6 to 6
- key_rope: bfloat16 [1024, 64], P('ctx'), may hold values from -10 to 10
- w_uk: bfloat16 [512, 16384], P(None, 'head'), may hold values from -0.25 to 0.25
- w_uv: bfloat16 [512, 16384], P(None, 'head'), may hold values from -0.25 to 0.25
- d_out: bfloat16 [1024, 16384], P('ctx', 'head'), may hold values from -0.29882812 to 0.29882812
- block_mask: int32 [8, 8], replicated, may hold values from 0 to 1, as said below
Outputs:
- grad_steer: float32 [8, 24576], P('ctx', 'head')
- grad_latent_bias: float32 [8, 1536], P('ctx')
The draws below stay inside these ranges and needn't reach their ends.
Inputs may be any that keep to these rules, and one draw needn't show every extreme that they name: `block_mask`: query block i always attends key block i; its other entries are 1 at a rate drawn per query block among 1/16, 2/16, 4/16 and 7/16.
All inputs are finite; a program needn't handle non-finite values.
Results may differ from the reference program's by a relative error of at most 0.024.
Values may be sent and summed in bfloat16 or wider, within the bound.
No kernel may reach another device: no remote copies, remote signals or barrier semaphores. Data moves between devices by JAX's collectives and lax.ppermute only.
A program may use at most 128 MiB of HBM per device.

```python
import jax
import jax.numpy as jnp
from jax import lax

H = 128
QL = 1536
KVL = 512
NOPE = 128
ROPE = 64
VD = 128
BLK = 128
QUERIES = 1024
KEYS = 1024
QB = 8
KB = 8


def draw_block_mask(key, part):
    first_key, second_key = jax.random.split(key)
    level = jax.random.randint(first_key, (QB, 1), 0, 4)
    rate = 1 + level * (level + 1) // 2
    rolls = jax.random.randint(second_key, (QB, KB), 0, 16)
    own_col = (jnp.arange(QB, dtype=jnp.int32) * KB // QB)[:, None]
    columns = jnp.arange(KB, dtype=jnp.int32)[None, :]
    return jnp.where((rolls < rate) | (columns == own_col), 1, 0).astype(jnp.int32)


def draw_steer(key, part):
    first_key = jax.random.fold_in(key, 0)
    head_width = NOPE + ROPE
    values = jnp.clip(0.5 * jax.random.normal(first_key, (QB, H, head_width), jnp.float32), -2.5, 2.5)
    return values.reshape(QB, H * head_width).astype(jnp.float32)


def draw_key_rope(key, part):
    first_key = jax.random.fold_in(key, 0)
    values = jnp.clip(jax.random.normal(first_key, (KEYS, ROPE), jnp.float32), -4.0, 4.0)
    return values.astype(jnp.bfloat16)


def shard_levels(own_key, dims, pieces, least, high):
    factor_of = 1.0
    for position, parts in pieces:
        draws = jax.random.uniform(jax.random.fold_in(jax.random.fold_in(own_key, 6), position), (parts,), jnp.float32, least / len(pieces), high / len(pieces))
        factor_of = factor_of * jnp.repeat(jnp.exp(draws), dims[position] // parts).reshape((-1,) + (1,) * (len(dims) - 1 - position))
    return factor_of


def scatter_about(rng, dims, scale, limit, pieces=(), kind=jnp.bfloat16):
    entries = scale * jax.random.normal(rng, dims, jnp.float32)
    if pieces:
        entries = entries * shard_levels(rng, dims, pieces, -0.22, 0.18)
    return jnp.clip(entries, -limit, limit).astype(kind)


def setup_inputs(seed: int = 0) -> dict:
    splits = jax.random.split(jax.random.key(seed), 12)
    q_latent = scatter_about(splits[0], (QUERIES, QL), 1.0, 6.0, ((0, 8),))
    latent_bias = scatter_about(splits[1], (QB, QL), 0.5, 3.0, ((0, 8),), jnp.float32)
    norm_gain = jnp.clip(1.0 + 0.1 * jax.random.normal(splits[2], (QL,), jnp.float32), 0.5, 1.5)
    w_q = scatter_about(splits[3], (QL, H * (NOPE + ROPE)), QL ** -0.5, 0.15625, ((0, 8), (1, 4)))
    steer = draw_steer(jax.random.fold_in(splits[11], 71), 0)
    kv_latent = scatter_about(splits[5], (KEYS, KVL), 1.0, 6.0, ((0, 8),))
    key_rope = draw_key_rope(jax.random.fold_in(splits[11], 71), 0)
    w_uk = scatter_about(splits[7], (KVL, H * NOPE), KVL ** -0.5, 0.25, ((1, 4),))
    w_uv = scatter_about(splits[8], (KVL, H * VD), KVL ** -0.5, 0.25, ((1, 4),))
    d_out = scatter_about(splits[9], (QUERIES, H * VD), 0.05, 0.29882812, ((0, 8), (1, 4)))
    block_mask = draw_block_mask(jax.random.fold_in(splits[11], 71), 0)
    return {"q_latent": q_latent, "latent_bias": latent_bias, "norm_gain": norm_gain, "w_q": w_q, "steer": steer, "kv_latent": kv_latent, "key_rope": key_rope, "w_uk": w_uk, "w_uv": w_uv, "d_out": d_out, "block_mask": block_mask}


epsilon = 1e-06

def rounded(values):
    return lax.optimization_barrier(values.astype(jnp.bfloat16)).astype(jnp.float32)

def reference(q_latent, latent_bias, norm_gain, w_q, steer, kv_latent, key_rope, w_uk, w_uv, d_out, block_mask):
    head_width = NOPE + ROPE
    score_scale = head_width ** (-0.5)
    row_count = BLK * H
    highest = lax.Precision.HIGHEST
    lat_blocks = kv_latent.astype(jnp.float32).reshape(KB, BLK, KVL)
    rope_blocks = key_rope.astype(jnp.float32).reshape(KB, BLK, ROPE)
    wq_full = w_q.astype(jnp.float32)
    key_up = w_uk.astype(jnp.float32).reshape(KVL, H, NOPE)
    value_up = w_uv.astype(jnp.float32).reshape(KVL, H, VD)

    def one_block(index):
        latent_rows = lax.dynamic_slice_in_dim(q_latent, index * BLK, BLK, 0).astype(jnp.float32)
        shifted = latent_rows + lax.dynamic_slice_in_dim(latent_bias, index, 1, 0)
        inv_rms = lax.rsqrt(lax.optimization_barrier(jnp.mean(shifted * shifted, axis=1, keepdims=True)) + epsilon)
        normed = shifted * inv_rms
        c_query = rounded(normed * norm_gain)
        projected = jnp.dot(c_query, wq_full, precision=highest, preferred_element_type=jnp.float32)
        query_all = rounded(projected + lax.dynamic_slice_in_dim(steer, index, 1, 0)).reshape(BLK, H, head_width)
        q_absorbed = rounded(jnp.einsum('qhn,khn->qhk', query_all[:, :, :NOPE], key_up, precision=highest)).reshape(row_count, KVL)
        q_rope = query_all[:, :, NOPE:].reshape(row_count, ROPE)
        grad_out = lax.dynamic_slice_in_dim(d_out, index * BLK, BLK, 0).astype(jnp.float32).reshape(BLK, H, VD)
        g_absorbed = rounded(jnp.einsum('qhv,khv->qhk', grad_out, value_up, precision=highest)).reshape(row_count, KVL)
        mask_row = lax.dynamic_index_in_dim(block_mask, index, 0, keepdims=False)

        def visit_block(status, inputs):
            lat_tile, rope_tile, flag = inputs

            def update(status):
                peak, total_weight, weighted, lat_acc, rope_acc = status
                scores = (jnp.dot(q_absorbed, lat_tile.T, precision=highest) + jnp.dot(q_rope, rope_tile.T, precision=highest)) * score_scale
                new_peak = jnp.maximum(peak, lax.optimization_barrier(jnp.max(scores, axis=1)))
                factor = jnp.exp(peak - new_peak)
                weights = jnp.exp(scores - new_peak[:, None])
                dots = jnp.dot(g_absorbed, lat_tile.T, precision=highest)
                mixed = weights * dots
                total_weight = total_weight * factor + lax.optimization_barrier(jnp.sum(weights, axis=1))
                weighted = weighted * factor + lax.optimization_barrier(jnp.sum(mixed, axis=1))
                stacked = rounded(jnp.concatenate([mixed, weights], axis=0))
                doubled = jnp.concatenate([factor, factor])[:, None]
                lat_acc = lat_acc * doubled + jnp.dot(stacked, lat_tile, precision=highest)
                rope_acc = rope_acc * doubled + jnp.dot(stacked, rope_tile, precision=highest)
                return (new_peak, total_weight, weighted, lat_acc, rope_acc)

            def keep_status(status):
                return status
            return (lax.cond(flag > 0, update, keep_status, status), None)
        start_status = (jnp.full((row_count,), -1e+30, jnp.float32), jnp.zeros((row_count,), jnp.float32), jnp.zeros((row_count,), jnp.float32), jnp.zeros((2 * row_count, KVL), jnp.float32), jnp.zeros((2 * row_count, ROPE), jnp.float32))
        final, unused = lax.scan(visit_block, start_status, (lat_blocks, rope_blocks, mask_row))
        peak, total_weight, weighted, lat_acc, rope_acc = final
        ratio = (weighted / total_weight)[:, None]
        inverse = (score_scale / total_weight)[:, None]
        grad_lat = rounded((lat_acc[:row_count] - ratio * lat_acc[row_count:]) * inverse)
        grad_rope = (rope_acc[:row_count] - ratio * rope_acc[row_count:]) * inverse
        grad_nope = jnp.einsum('qhk,khn->qhn', grad_lat.reshape(BLK, H, KVL), key_up, precision=highest)
        grad_query = jnp.concatenate([grad_nope, grad_rope.reshape(BLK, H, ROPE)], axis=2).reshape(BLK, H * head_width)
        steer_grad = lax.optimization_barrier(jnp.sum(grad_query, axis=0))
        latent_grad = jnp.dot(rounded(grad_query), wq_full.T, precision=highest)
        scaled = latent_grad * norm_gain
        project_mean = lax.optimization_barrier(jnp.mean(scaled * normed, axis=1, keepdims=True))
        grad_shifted = inv_rms * (scaled - normed * project_mean)
        return (steer_grad, lax.optimization_barrier(jnp.sum(grad_shifted, axis=0)))
    grad_steer, grad_latent_bias = lax.map(one_block, jnp.arange(QB, dtype=jnp.int32))
    return (grad_steer, grad_latent_bias)
```

```python
import math

import jax
import jax.numpy as jnp
from jax import lax
from jax.experimental import pallas as pl
from jax.experimental.pallas import tpu as pltpu
from jax.sharding import PartitionSpec as P

KVL = 512
NOPE = 128
ROPE = 64
VD = 128
BLK = 128


epsilon = 1e-06
lowest = -1e30


def contract_last(left, right):
    return lax.dot_general(
        left, right, (((1,), (1,)), ((), ())), preferred_element_type=jnp.float32
    )


def shards(
    q_latent, latent_bias, norm_gain, w_q, steer, kv_latent, key_rope, w_uk, w_uv, d_out, block_mask
):
    queries = q_latent.shape[0]
    nblocks = queries // BLK
    head_count = w_uk.shape[1] // NOPE
    head_width = NOPE + ROPE
    score_scale = head_width ** (-0.5)
    row_count = queries * head_count
    shifted = q_latent.astype(jnp.float32) + jnp.repeat(latent_bias, BLK, axis=0)
    inv_rms = lax.rsqrt(jnp.mean(shifted * shifted, axis=1, keepdims=True) + epsilon)
    normed = shifted * inv_rms
    c_query = (normed * norm_gain).astype(jnp.bfloat16)
    full_wq = lax.all_gather(w_q, "ctx", axis=0, tiled=True)
    projected = jnp.dot(c_query, full_wq, preferred_element_type=jnp.float32)
    query_all = (
        (projected + jnp.repeat(steer, BLK, axis=0))
        .astype(jnp.bfloat16)
        .reshape(queries, head_count, head_width)
    )
    q_rope = query_all[:, :, NOPE:].reshape(row_count, ROPE)
    key_up = w_uk.reshape(KVL, head_count, NOPE)
    value_up = w_uv.reshape(KVL, head_count, VD)
    q_absorbed = (
        jnp.einsum(
            "qhn,khn->qhk", query_all[:, :, :NOPE], key_up, preferred_element_type=jnp.float32
        )
        .astype(jnp.bfloat16)
        .reshape(row_count, KVL)
    )
    g_absorbed = (
        jnp.einsum(
            "qhv,khv->qhk",
            d_out.reshape(queries, head_count, VD),
            value_up,
            preferred_element_type=jnp.float32,
        )
        .astype(jnp.bfloat16)
        .reshape(row_count, KVL)
    )
    my_mask = lax.dynamic_slice_in_dim(block_mask, lax.axis_index("ctx") * nblocks, nblocks, 0)
    start_status = (
        jnp.full((row_count,), lowest, jnp.float32),
        jnp.zeros((row_count,), jnp.float32),
        jnp.zeros((row_count,), jnp.float32),
        jnp.zeros((2 * row_count, KVL), jnp.float32),
        jnp.zeros((2 * row_count, ROPE), jnp.float32),
    )
    lat_portion = lax.all_gather(kv_latent, "ctx", axis=0, tiled=True)
    rope_portion = lax.all_gather(key_rope, "ctx", axis=0, tiled=True)
    key_total = lat_portion.shape[0]
    tile_len = math.gcd(key_total, BLK)
    tile_count = key_total // tile_len

    def visit_tile(status, inputs):
        lat_tile, rope_tile, offset = inputs
        key_block = offset * tile_len // BLK
        column = lax.dynamic_index_in_dim(my_mask, key_block, 1, keepdims=False)

        def update(status):
            peak, total_weight, weighted, lat_acc, rope_acc = status
            live_rows = jnp.repeat(column > 0, head_count * BLK)[:, None]
            scores = (
                contract_last(q_absorbed, lat_tile) + contract_last(q_rope, rope_tile)
            ) * score_scale
            scores = jnp.where(live_rows, scores, lowest)
            new_peak = jnp.maximum(peak, jnp.max(scores, axis=1))
            factor = jnp.exp(peak - new_peak)
            weights = jnp.where(live_rows, jnp.exp(scores - new_peak[:, None]), 0.0)
            dots = contract_last(g_absorbed, lat_tile)
            mixed = weights * dots
            total_weight = total_weight * factor + jnp.sum(weights, axis=1)
            weighted = weighted * factor + jnp.sum(mixed, axis=1)
            stacked = jnp.concatenate([mixed, weights], axis=0).astype(jnp.bfloat16)
            doubled = jnp.concatenate([factor, factor])[:, None]
            lat_acc = lat_acc * doubled + jnp.dot(
                stacked, lat_tile, preferred_element_type=jnp.float32
            )
            rope_acc = rope_acc * doubled + jnp.dot(
                stacked, rope_tile, preferred_element_type=jnp.float32
            )
            return (new_peak, total_weight, weighted, lat_acc, rope_acc)

        def keep_status(status):
            return status

        return (lax.cond(jnp.max(column) > 0, update, keep_status, status), None)

    offsets = jnp.arange(tile_count, dtype=jnp.int32)
    tiles = (
        lat_portion.reshape(tile_count, tile_len, KVL),
        rope_portion.reshape(tile_count, tile_len, ROPE),
        offsets,
    )
    result, unused = lax.scan(visit_tile, start_status, tiles)
    peak, total_weight, weighted, lat_acc, rope_acc = result
    ratio = (weighted / total_weight)[:, None]
    inverse = (score_scale / total_weight)[:, None]
    grad_lat = ((lat_acc[:row_count] - ratio * lat_acc[row_count:]) * inverse).astype(jnp.bfloat16)
    grad_rope = (rope_acc[:row_count] - ratio * rope_acc[row_count:]) * inverse
    grad_nope = jnp.einsum(
        "qhk,khn->qhn",
        grad_lat.reshape(queries, head_count, KVL),
        key_up,
        preferred_element_type=jnp.float32,
    )
    grad_query = jnp.concatenate(
        [grad_nope, grad_rope.reshape(queries, head_count, ROPE)], axis=2
    ).reshape(queries, head_count * head_width)
    grad_steer = jnp.sum(grad_query.reshape(nblocks, BLK, head_count * head_width), axis=1)
    grad_round = grad_query.astype(jnp.bfloat16)
    partial_grad = contract_last(grad_round, full_wq)
    latent_grad = lax.psum(partial_grad.astype(jnp.bfloat16), "head").astype(jnp.float32)
    scaled = latent_grad * norm_gain
    project_mean = jnp.mean(scaled * normed, axis=1, keepdims=True)
    grad_shifted = inv_rms * (scaled - normed * project_mean)
    grad_bias = jnp.sum(grad_shifted.reshape(nblocks, BLK, grad_shifted.shape[1]), axis=1)
    return (grad_steer, grad_bias)


WIDE = 256
PIECE = 32
VMEM_LIMIT = 60 * 1024 * 1024
f32 = jnp.float32
bf16 = jnp.bfloat16


def dot(left, right):
    return jnp.dot(left, right, preferred_element_type=f32)


def prep_kernel(pick, lat_ref, bias_ref, gain_ref, kv_ref, rope_ref, out_ref):
    ql = lat_ref.shape[1]
    shifted = lat_ref[...].astype(f32) + bias_ref[...]
    inv = lax.rsqrt(jnp.mean(shifted * shifted, axis=1, keepdims=True) + epsilon)
    out_ref[:, :ql] = (shifted * inv * gain_ref[...]).astype(bf16)
    out_ref[:, ql : ql + KVL] = kv_ref[...]
    out_ref[:, ql + KVL : ql + KVL + ROPE] = rope_ref[...]
    high = inv.astype(bf16)
    low = (inv - high.astype(f32)).astype(bf16)
    lane = lax.broadcasted_iota(jnp.int32, (lat_ref.shape[0], ROPE), 1)
    pair = jnp.where(lane == 0, high.astype(f32), jnp.where(lane == 1, low.astype(f32), 0.0))
    out_ref[:, ql + KVL + ROPE :] = pair.astype(bf16)


def keys_kernel(place, near_ref, far_ref, uk_ref, uv_ref, c_ref, tail_ref, wide_ref, value_ref, kv_ref):
    ql = c_ref.shape[1]
    for position, ref in ((0, near_ref), (1, far_ref)):
        for piece in range(16):
            rows = pl.ds(pl.multiple_of(place[position * 16 + piece], PIECE), PIECE)
            c_ref[rows, :] = ref[piece, :, :ql]
            kv_ref[rows, :] = ref[piece, :, ql : ql + KVL]
            tail_ref[rows, :] = ref[piece, :, ql + KVL :]
    heads = wide_ref.shape[0]
    step = 256
    lane = lax.broadcasted_iota(jnp.int32, (step, NOPE), 1)
    for start in range(0, c_ref.shape[0], step):
        rows = slice(start, start + step)
        kv = kv_ref[rows, :]
        up = dot(kv, uk_ref[...])
        value_ref[rows, :] = dot(kv, uv_ref[...]).astype(bf16)
        rope = jnp.where(lane < ROPE, tail_ref[rows, :].astype(f32), 0.0)
        for head in range(heads):
            full = jnp.concatenate([up[:, head * NOPE : (head + 1) * NOPE], rope], axis=1)
            if head % 2:
                full = pltpu.roll(full, ROPE, 1)
            wide_ref[head, rows, :] = full.astype(bf16)


def query_kernel(place, *refs):
    count = len(refs) - 5
    weights, (c_ref, steer_ref, q_ref, proj_ref, full_ref) = refs[:count], refs[count:]
    depth = weights[0].shape[0]
    for index, ref in enumerate(weights):
        full_ref[pl.ds(pl.multiple_of(place[index] * depth, 64), depth), :] = ref[...]
    step = 256
    for start in range(0, c_ref.shape[0], step):
        projected = dot(c_ref[start : start + step, :], full_ref[...])
        proj_ref[start : start + step, :] = projected
        for part in range(step // BLK):
            block = start // BLK + part
            low = part * BLK
            q_ref[start + low : start + low + BLK, :] = (
                projected[low : low + BLK] + steer_ref[block : block + 1, :]
            ).astype(bf16)


def attend_kernel(mask, place, *refs):
    count = len(refs) - 16
    cots = refs[:count]
    (
        q_ref, proj_ref, tail_ref, wide_ref, value_ref, weight_ref, out_ref,
        cot_ref, sums_ref, weighted_ref, grad_ref, peak_ref, total_ref, mixed_ref, lat_ref, row_ref,
    ) = refs[count:]
    nblocks = count
    heads = wide_ref.shape[0]
    width = NOPE + ROPE
    scale = width ** (-0.5)
    for index, ref in enumerate(cots):
        cot_ref[place[index]] = ref[...]

    def block_step(block, carry):
        rows = pl.ds(pl.multiple_of(block * BLK, BLK), BLK)
        peak_ref[...] = jnp.full_like(peak_ref, lowest)
        total_ref[...] = jnp.zeros_like(total_ref)
        mixed_ref[...] = jnp.zeros_like(mixed_ref)
        lat_ref[...] = jnp.zeros_like(lat_ref)

        def key_step(key, inner):
            @pl.when(mask[block, key] > 0)
            def live():
                keys = pl.ds(pl.multiple_of(key * BLK, BLK), BLK)
                for head in range(heads):
                    left = head // 2 * 2 * width + head % 2 * NOPE
                    wide = wide_ref[head, keys, :]
                    scores = contract_last(q_ref[rows, left : left + WIDE], wide) * scale
                    dots = contract_last(
                        cot_ref[block, :, head * VD : (head + 1) * VD],
                        value_ref[keys, head * VD : (head + 1) * VD],
                    )
                    peak = peak_ref[head]
                    fresh = jnp.maximum(peak, jnp.max(scores, axis=1, keepdims=True))
                    factor = jnp.exp(peak - fresh)
                    weights = jnp.exp(scores - fresh)
                    mixed = weights * dots
                    peak_ref[head] = fresh
                    total_ref[head] = total_ref[head] * factor + jnp.sum(weights, axis=1, keepdims=True)
                    mixed_ref[head] = mixed_ref[head] * factor + jnp.sum(mixed, axis=1, keepdims=True)
                    stacked = jnp.concatenate([mixed, weights], axis=0).astype(bf16)
                    gained = dot(stacked, wide)
                    lat_ref[head, :BLK] = lat_ref[head, :BLK] * factor + gained[:BLK]
                    lat_ref[head, BLK:] = lat_ref[head, BLK:] * factor + gained[BLK:]

            return inner

        lax.fori_loop(0, mask.shape[1], key_step, 0)
        tail = tail_ref[rows, :].astype(f32)
        inv = tail[:, ROPE : ROPE + 1] + tail[:, ROPE + 1 : ROPE + 2]
        for pair in range(heads // 2):
            parts = []
            for head in (2 * pair, 2 * pair + 1):
                ratio = mixed_ref[head] / total_ref[head]
                parts.append((lat_ref[head, :BLK] - ratio * lat_ref[head, BLK:]) * (scale / total_ref[head]))
            left = pair * 2 * width
            grad_ref[:, left : left + 128] = parts[0][:, :128]
            grad_ref[:, left + 128 : left + 256] = parts[0][:, 128:] + parts[1][:, :128]
            grad_ref[:, left + 256 : left + 384] = parts[1][:, 128:]
        grad = grad_ref[...]
        sums_ref[pl.ds(block, 1), :] = jnp.sum(grad, axis=0, keepdims=True)
        weighted_ref[pl.ds(block, 1), :] = jnp.sum(grad * inv, axis=0, keepdims=True)
        products = grad * proj_ref[rows, :]
        row_ref[pl.ds(block, 1), :] = jnp.sum(products.T, axis=0, keepdims=True)
        return carry

    lax.fori_loop(0, nblocks, block_step, 0)
    weighted = weighted_ref[...]
    high = weighted.astype(bf16)
    low = (weighted - high.astype(f32)).astype(bf16)
    back = contract_last(high, weight_ref[...]) + contract_last(low, weight_ref[...])
    out_ref[...] = jnp.zeros_like(out_ref)
    chunks = []
    for array in (back, row_ref[...], sums_ref[...]):
        for start in range(0, array.shape[1], 128):
            chunks.append(array[:, start : start + 128])
    for index, chunk in enumerate(chunks):
        for block in range(nblocks):
            out_ref[block, index : index + 1, :] = chunk[block : block + 1, :]


def full(shape):
    return pl.BlockSpec(shape, lambda *unused: (0,) * len(shape))


def params():
    return pltpu.CompilerParams(vmem_limit_bytes=VMEM_LIMIT)


def cost(flops, moved):
    return pl.CostEstimate(flops=flops, bytes_accessed=moved, transcendentals=0)


def spread(
    ring, head_shards, q_latent, latent_bias, norm_gain, w_q, steer, kv_latent, key_rope, w_uk, w_uv, d_out, block_mask
):
    ql = q_latent.shape[1]
    queries = ring * BLK
    mine = lax.axis_index("ctx")
    lane = lax.axis_index("head")
    columns = w_q.shape[1] // ring
    cot_columns = d_out.shape[1] // ring
    heads = cot_columns // VD
    shifts = range(1, ring)

    def chunk(array, width, step):
        return lax.dynamic_slice_in_dim(array, (mine + step) % ring * width, width, 1)

    def turn(array, step):
        return lax.ppermute(array, "ctx", [(i, (i + step) % ring) for i in range(ring)])

    gain_row = norm_gain[None, :]
    payload_width = ql + KVL + 2 * ROPE
    piece = pl.pallas_call(
        prep_kernel,
        out_shape=jax.ShapeDtypeStruct((PIECE, payload_width), bf16),
        grid_spec=pltpu.PrefetchScalarGridSpec(
            num_scalar_prefetch=1,
            grid=(1,),
            in_specs=[
                pl.BlockSpec((PIECE, ql), lambda i, pick: (pick[0], 0)),
                full((1, ql)),
                full((1, ql)),
                pl.BlockSpec((PIECE, KVL), lambda i, pick: (pick[0], 0)),
                pl.BlockSpec((PIECE, ROPE), lambda i, pick: (pick[0], 0)),
            ],
            out_specs=full((PIECE, payload_width)),
        ),
        cost_estimate=cost(10**6, 10**6),
    )(lane[None], q_latent, latent_bias, gain_row, kv_latent, key_rope)
    pieces = [piece] + [turn(piece, 2 * step) for step in range(1, ring // 2)]
    weight_parts = [chunk(w_q, columns, 0)] + [turn(chunk(w_q, columns, step), step) for step in shifts]
    first = jnp.stack(pieces)
    second = lax.ppermute(first, "ctx", [(i, i ^ 1) for i in range(ring)])
    both = jnp.concatenate([first, second])
    other = lax.ppermute(both, "head", [(i, i ^ 2) for i in range(head_shards)])
    near = jnp.concatenate([both, other])
    far = lax.ppermute(near, "head", [(i, i ^ 1) for i in range(head_shards)])
    cot_parts = [chunk(d_out, cot_columns, 0)] + [turn(chunk(d_out, cot_columns, step), step) for step in shifts]
    all_steer = lax.all_to_all(steer.reshape(ring, columns), "ctx", 0, 0, tiled=True)

    z, x = mine // 2, mine % 2
    places = []
    for core in range(2):
        for y in range(2):
            for dx in range(2):
                for step in range(ring // 2):
                    block = (z + ring // 2 - step) % (ring // 2) * 2 + (x + dx) % 2
                    places.append(block * BLK + PIECE * (lane ^ (2 * y + core)))
    places = jnp.stack(places).astype(jnp.int32)
    sources = jnp.stack([(mine + ring - step) % ring for step in range(ring)]).astype(jnp.int32)

    c_query, tail, wide, values = pl.pallas_call(
        keys_kernel,
        out_shape=(
            jax.ShapeDtypeStruct((queries, ql), bf16),
            jax.ShapeDtypeStruct((queries, 2 * ROPE), bf16),
            jax.ShapeDtypeStruct((heads, queries, WIDE), bf16),
            jax.ShapeDtypeStruct((queries, heads * VD), bf16),
        ),
        grid_spec=pltpu.PrefetchScalarGridSpec(
            num_scalar_prefetch=1,
            grid=(1,),
            in_specs=[
                full((16, PIECE, payload_width)),
                full((16, PIECE, payload_width)),
                pl.BlockSpec((KVL, heads * NOPE), lambda i, place: (0, place[32])),
                pl.BlockSpec((KVL, heads * VD), lambda i, place: (0, place[32])),
            ],
            out_specs=(
                full((queries, ql)),
                full((queries, 2 * ROPE)),
                full((heads, queries, WIDE)),
                full((queries, heads * VD)),
            ),
            scratch_shapes=[pltpu.VMEM((queries, KVL), bf16)],
        ),
        compiler_params=params(),
        cost_estimate=cost(2 * 10**9, 10**7),
    )(jnp.concatenate([places, mine[None]]), near, far, w_uk, w_uv)

    query, projected, weight = pl.pallas_call(
        query_kernel,
        out_shape=(
            jax.ShapeDtypeStruct((queries, columns), bf16),
            jax.ShapeDtypeStruct((queries, columns), f32),
            jax.ShapeDtypeStruct((ql, columns), bf16),
        ),
        grid_spec=pltpu.PrefetchScalarGridSpec(
            num_scalar_prefetch=1,
            grid=(1,),
            in_specs=[full(weight_parts[0].shape)] * ring + [full((queries, ql)), full((ring, columns))],
            out_specs=(full((queries, columns)), full((queries, columns)), full((ql, columns))),
        ),
        compiler_params=params(),
        cost_estimate=cost(3 * 10**9, 10**7),
    )(sources, *weight_parts, c_query, all_steer)

    used = (ql + BLK + columns) // 128
    slots = (used + 7) // 8 * 8
    sums = pl.pallas_call(
        attend_kernel,
        out_shape=jax.ShapeDtypeStruct((ring, slots, 128), f32),
        grid_spec=pltpu.PrefetchScalarGridSpec(
            num_scalar_prefetch=2,
            grid=(1,),
            in_specs=[full((BLK, cot_columns))] * ring
            + [
                full((queries, columns)),
                full((queries, columns)),
                full((queries, 2 * ROPE)),
                full((heads, queries, WIDE)),
                full((queries, heads * VD)),
                full((ql, columns)),
            ],
            out_specs=full((ring, slots, 128)),
            scratch_shapes=[
                pltpu.VMEM((ring, BLK, cot_columns), bf16),
                pltpu.VMEM((ring, columns), f32),
                pltpu.VMEM((ring, columns), f32),
                pltpu.VMEM((BLK, columns), f32),
                pltpu.VMEM((heads, BLK, 1), f32),
                pltpu.VMEM((heads, BLK, 1), f32),
                pltpu.VMEM((heads, BLK, 1), f32),
                pltpu.VMEM((heads, 2 * BLK, WIDE), f32),
                pltpu.VMEM((ring, BLK), f32),
            ],
        ),
        compiler_params=params(),
        cost_estimate=cost(8 * 10**9, 10**7),
    )(block_mask, sources, *cot_parts, query, projected, tail, wide, values, weight)

    arrived = lax.all_to_all(sums, "ctx", 0, 0, tiled=True)
    cut = (ql + BLK) // 128
    grad_steer = arrived[:, cut:used].reshape(1, ring * columns)
    local = jnp.sum(arrived[:, :cut], axis=0)
    summed = local
    for bits in range(1, head_shards):
        summed = summed + lax.ppermute(local, "head", [(i, i ^ bits) for i in range(head_shards)])
    back = summed[: ql // 128].reshape(1, ql)
    dots = summed[ql // 128 : cut].reshape(BLK, 1)
    shifted = q_latent.astype(f32) + latent_bias
    inv = lax.rsqrt(jnp.mean(shifted * shifted, axis=1, keepdims=True) + epsilon)
    pull = jnp.sum(shifted * (inv * inv * dots / ql), axis=0, keepdims=True)
    return (grad_steer, back * gain_row - pull)


def solution(mesh):
    ring, head_shards = mesh.shape["ctx"], mesh.shape["head"]

    def body(*arrays):
        heads = arrays[7].shape[1] // NOPE
        fits = arrays[0].shape[0] == BLK and ring == 8 and head_shards == 4 and heads % (2 * ring) == 0
        if fits:
            return spread(ring, head_shards, *arrays)
        return shards(*arrays)

    in_specs = (
        P("ctx", None),
        P("ctx", None),
        P(),
        P("ctx", "head"),
        P("ctx", "head"),
        P("ctx", None),
        P("ctx", None),
        P(None, "head"),
        P(None, "head"),
        P("ctx", "head"),
        P(),
    )
    out_specs = (P("ctx", "head"), P("ctx", None))
    return jax.shard_map(body, mesh=mesh, in_specs=in_specs, out_specs=out_specs, check_vma=False)
```

```python
import math

import jax
import jax.numpy as jnp
from jax import lax
from jax.experimental import pallas as pl
from jax.experimental.pallas import tpu as pltpu
from jax.sharding import PartitionSpec as P

KVL = 512
NOPE = 128
ROPE = 64
VD = 128
BLK = 128


epsilon = 1e-06
lowest = -1e30


def contract_last(left, right):
    return lax.dot_general(
        left, right, (((1,), (1,)), ((), ())), preferred_element_type=jnp.float32
    )


def shards(
    q_latent, latent_bias, norm_gain, w_q, steer, kv_latent, key_rope, w_uk, w_uv, d_out, block_mask
):
    queries = q_latent.shape[0]
    nblocks = queries // BLK
    head_count = w_uk.shape[1] // NOPE
    head_width = NOPE + ROPE
    score_scale = head_width ** (-0.5)
    row_count = queries * head_count
    shifted = q_latent.astype(jnp.float32) + jnp.repeat(latent_bias, BLK, axis=0)
    inv_rms = lax.rsqrt(jnp.mean(shifted * shifted, axis=1, keepdims=True) + epsilon)
    normed = shifted * inv_rms
    c_query = (normed * norm_gain).astype(jnp.bfloat16)
    full_wq = lax.all_gather(w_q, "ctx", axis=0, tiled=True)
    projected = jnp.dot(c_query, full_wq, preferred_element_type=jnp.float32)
    query_all = (
        (projected + jnp.repeat(steer, BLK, axis=0))
        .astype(jnp.bfloat16)
        .reshape(queries, head_count, head_width)
    )
    q_rope = query_all[:, :, NOPE:].reshape(row_count, ROPE)
    key_up = w_uk.reshape(KVL, head_count, NOPE)
    value_up = w_uv.reshape(KVL, head_count, VD)
    q_absorbed = (
        jnp.einsum(
            "qhn,khn->qhk", query_all[:, :, :NOPE], key_up, preferred_element_type=jnp.float32
        )
        .astype(jnp.bfloat16)
        .reshape(row_count, KVL)
    )
    g_absorbed = (
        jnp.einsum(
            "qhv,khv->qhk",
            d_out.reshape(queries, head_count, VD),
            value_up,
            preferred_element_type=jnp.float32,
        )
        .astype(jnp.bfloat16)
        .reshape(row_count, KVL)
    )
    my_mask = lax.dynamic_slice_in_dim(block_mask, lax.axis_index("ctx") * nblocks, nblocks, 0)
    start_status = (
        jnp.full((row_count,), lowest, jnp.float32),
        jnp.zeros((row_count,), jnp.float32),
        jnp.zeros((row_count,), jnp.float32),
        jnp.zeros((2 * row_count, KVL), jnp.float32),
        jnp.zeros((2 * row_count, ROPE), jnp.float32),
    )
    lat_portion = lax.all_gather(kv_latent, "ctx", axis=0, tiled=True)
    rope_portion = lax.all_gather(key_rope, "ctx", axis=0, tiled=True)
    key_total = lat_portion.shape[0]
    tile_len = math.gcd(key_total, BLK)
    tile_count = key_total // tile_len

    def visit_tile(status, inputs):
        lat_tile, rope_tile, offset = inputs
        key_block = offset * tile_len // BLK
        column = lax.dynamic_index_in_dim(my_mask, key_block, 1, keepdims=False)

        def update(status):
            peak, total_weight, weighted, lat_acc, rope_acc = status
            live_rows = jnp.repeat(column > 0, head_count * BLK)[:, None]
            scores = (
                contract_last(q_absorbed, lat_tile) + contract_last(q_rope, rope_tile)
            ) * score_scale
            scores = jnp.where(live_rows, scores, lowest)
            new_peak = jnp.maximum(peak, jnp.max(scores, axis=1))
            factor = jnp.exp(peak - new_peak)
            weights = jnp.where(live_rows, jnp.exp(scores - new_peak[:, None]), 0.0)
            dots = contract_last(g_absorbed, lat_tile)
            mixed = weights * dots
            total_weight = total_weight * factor + jnp.sum(weights, axis=1)
            weighted = weighted * factor + jnp.sum(mixed, axis=1)
            stacked = jnp.concatenate([mixed, weights], axis=0).astype(jnp.bfloat16)
            doubled = jnp.concatenate([factor, factor])[:, None]
            lat_acc = lat_acc * doubled + jnp.dot(
                stacked, lat_tile, preferred_element_type=jnp.float32
            )
            rope_acc = rope_acc * doubled + jnp.dot(
                stacked, rope_tile, preferred_element_type=jnp.float32
            )
            return (new_peak, total_weight, weighted, lat_acc, rope_acc)

        def keep_status(status):
            return status

        return (lax.cond(jnp.max(column) > 0, update, keep_status, status), None)

    offsets = jnp.arange(tile_count, dtype=jnp.int32)
    tiles = (
        lat_portion.reshape(tile_count, tile_len, KVL),
        rope_portion.reshape(tile_count, tile_len, ROPE),
        offsets,
    )
    result, _ = lax.scan(visit_tile, start_status, tiles)
    _, total_weight, weighted, lat_acc, rope_acc = result
    ratio = (weighted / total_weight)[:, None]
    inverse = (score_scale / total_weight)[:, None]
    grad_lat = ((lat_acc[:row_count] - ratio * lat_acc[row_count:]) * inverse).astype(jnp.bfloat16)
    grad_rope = (rope_acc[:row_count] - ratio * rope_acc[row_count:]) * inverse
    grad_nope = jnp.einsum(
        "qhk,khn->qhn",
        grad_lat.reshape(queries, head_count, KVL),
        key_up,
        preferred_element_type=jnp.float32,
    )
    grad_query = jnp.concatenate(
        [grad_nope, grad_rope.reshape(queries, head_count, ROPE)], axis=2
    ).reshape(queries, head_count * head_width)
    grad_steer = jnp.sum(grad_query.reshape(nblocks, BLK, head_count * head_width), axis=1)
    grad_round = grad_query.astype(jnp.bfloat16)
    partial_grad = contract_last(grad_round, full_wq)
    latent_grad = lax.psum(partial_grad.astype(jnp.bfloat16), "head").astype(jnp.float32)
    scaled = latent_grad * norm_gain
    project_mean = jnp.mean(scaled * normed, axis=1, keepdims=True)
    grad_shifted = inv_rms * (scaled - normed * project_mean)
    grad_bias = jnp.sum(grad_shifted.reshape(nblocks, BLK, grad_shifted.shape[1]), axis=1)
    return (grad_steer, grad_bias)


WIDE = 256
PIECE = 32
UNROLL = 2
VMEM_LIMIT = 60 * 1024 * 1024
f32 = jnp.float32
bf16 = jnp.bfloat16


def dot(left, right):
    return jnp.dot(left, right, preferred_element_type=f32)


def prep_kernel(pick, lat_ref, bias_ref, gain_ref, kv_ref, rope_ref, out_ref):
    ql = lat_ref.shape[1]
    shifted = lat_ref[...].astype(f32) + bias_ref[...]
    inv = lax.rsqrt(jnp.mean(shifted * shifted, axis=1, keepdims=True) + epsilon)
    out_ref[:, :ql] = (shifted * inv * gain_ref[...]).astype(bf16)
    out_ref[:, ql : ql + KVL] = kv_ref[...]
    out_ref[:, ql + KVL : ql + KVL + ROPE] = rope_ref[...]
    high = inv.astype(bf16)
    low = (inv - high.astype(f32)).astype(bf16)
    lane = lax.broadcasted_iota(jnp.int32, (lat_ref.shape[0], ROPE), 1)
    pair = jnp.where(lane == 0, high.astype(f32), jnp.where(lane == 1, low.astype(f32), 0.0))
    out_ref[:, ql + KVL + ROPE :] = pair.astype(bf16)


def keys_kernel(place, near_ref, far_ref, uk_ref, uv_ref, c_ref, tail_ref, wide_ref, value_ref, kv_ref):
    ql = c_ref.shape[1]
    for position, ref in ((0, near_ref), (1, far_ref)):
        for piece in range(16):
            rows = pl.ds(pl.multiple_of(place[position * 16 + piece], PIECE), PIECE)
            c_ref[rows, :] = ref[piece, :, :ql]
            kv_ref[rows, :] = ref[piece, :, ql : ql + KVL]
            tail_ref[rows, :] = ref[piece, :, ql + KVL :]
    heads = wide_ref.shape[0]
    step = 256
    lane = lax.broadcasted_iota(jnp.int32, (step, NOPE), 1)
    for start in range(0, c_ref.shape[0], step):
        rows = slice(start, start + step)
        kv = kv_ref[rows, :]
        up = dot(kv, uk_ref[...])
        value_ref[rows, :] = dot(kv, uv_ref[...]).astype(bf16)
        rope = jnp.where(lane < ROPE, tail_ref[rows, :].astype(f32), 0.0)
        for head in range(heads):
            full = jnp.concatenate([up[:, head * NOPE : (head + 1) * NOPE], rope], axis=1)
            if head % 2:
                full = pltpu.roll(full, ROPE, 1)
            wide_ref[head, rows, :] = full.astype(bf16)


def query_kernel(place, *refs):
    count = len(refs) - 5
    weights, (c_ref, steer_ref, q_ref, proj_ref, full_ref) = refs[:count], refs[count:]
    depth = weights[0].shape[0]
    for index, ref in enumerate(weights):
        full_ref[pl.ds(pl.multiple_of(place[index] * depth, 64), depth), :] = ref[...]
    step = 256
    for start in range(0, c_ref.shape[0], step):
        projected = dot(c_ref[start : start + step, :], full_ref[...])
        proj_ref[start : start + step, :] = projected
        for part in range(step // BLK):
            block = start // BLK + part
            low = part * BLK
            q_ref[start + low : start + low + BLK, :] = (
                projected[low : low + BLK] + steer_ref[block : block + 1, :]
            ).astype(bf16)


def attend_kernel(mask, place, *refs):
    count = len(refs) - 17
    cots = refs[:count]
    (
        q_ref, proj_ref, tail_ref, wide_ref, value_ref, weight_ref, out_ref,
        cot_ref, sums_ref, weighted_ref, row_ref, score_ref, dot_ref, first_ref, second_ref, grad_ref, pair_ref,
    ) = refs[count:]
    nblocks = count
    heads = wide_ref.shape[0]
    width = NOPE + ROPE
    scale = width ** (-0.5)
    for index, ref in enumerate(cots):
        cot_ref[place[index]] = ref[...]

    def list_step(index, found):
        block, key = index // mask.shape[1], index % mask.shape[1]
        pair_ref[0, found] = block
        pair_ref[1, found] = key
        return found + (mask[block, key] > 0).astype(jnp.int32)

    found = lax.fori_loop(0, nblocks * mask.shape[1], list_step, 0)
    pair_ref[0, found] = nblocks
    pair_ref[1, found] = 0
    trips = (found + UNROLL - 1) // UNROLL

    def each_pair(visit):
        def trip(index, carry):
            for part in range(UNROLL):
                pair = index * UNROLL + part
                visit(pair, pair_ref[0, pair], pair_ref[1, pair])
            return carry

        lax.fori_loop(0, trips, trip, 0)

    def each_block(visit):
        def trip(block, carry):
            visit(block)
            return carry

        lax.fori_loop(0, nblocks, trip, 0)

    def span(block):
        return pl.ds(pl.multiple_of(block * BLK, BLK), BLK)

    first_ref[...] = jnp.full_like(first_ref, lowest)

    def score(pair, block, key):
        rows = span(jnp.minimum(block, nblocks - 1))
        for head in range(heads):
            left = head // 2 * 2 * width + head % 2 * NOPE
            scores = contract_last(q_ref[rows, left : left + WIDE], wide_ref[head, span(key), :]) * scale
            score_ref[pair, head] = scores
            first_ref[block, head] = jnp.maximum(first_ref[block, head], scores)

    each_pair(score)

    peak_ref = grad_ref

    def find_peak(block):
        for head in range(heads):
            peak = jnp.max(first_ref[block, head], axis=1, keepdims=True)
            peak_ref[block, :, head * BLK : (head + 1) * BLK] = jnp.broadcast_to(peak, (BLK, BLK))

    each_block(find_peak)
    peak_ref[nblocks] = jnp.zeros_like(peak_ref[nblocks])
    first_ref[...] = jnp.zeros_like(first_ref)
    second_ref[...] = jnp.zeros_like(second_ref)

    def weigh(pair, block, key):
        source = jnp.minimum(block, nblocks - 1)
        for head in range(heads):
            lanes = slice(head * VD, (head + 1) * VD)
            dots = contract_last(cot_ref[source, :, lanes], value_ref[span(key), lanes])
            weights = jnp.exp(score_ref[pair, head] - peak_ref[block, :, head * BLK : (head + 1) * BLK])
            score_ref[pair, head] = weights
            dot_ref[pair, head] = dots
            first_ref[block, head] = first_ref[block, head] + weights
            second_ref[block, head] = second_ref[block, head] + weights * dots

    each_pair(weigh)

    def normalise(block):
        for head in range(heads):
            total = jnp.sum(first_ref[block, head], axis=1, keepdims=True)
            mixed = jnp.sum(second_ref[block, head], axis=1, keepdims=True)
            first_ref[block, head] = jnp.broadcast_to(scale / total, (BLK, BLK))
            second_ref[block, head] = jnp.broadcast_to(mixed / total, (BLK, BLK))

    each_block(normalise)
    grad_ref[...] = jnp.zeros_like(grad_ref)

    def gather(pair, block, key):
        for head in range(heads):
            left = head // 2 * 2 * width + head % 2 * NOPE
            slope = score_ref[pair, head] * (dot_ref[pair, head] - second_ref[block, head])
            slope = (slope * first_ref[block, head]).astype(bf16)
            lanes = slice(left, left + WIDE)
            grad_ref[block, :, lanes] = grad_ref[block, :, lanes] + dot(slope, wide_ref[head, span(key), :])

    each_pair(gather)

    def reduce(block):
        grad = grad_ref[block]
        tail = tail_ref[span(block), :].astype(f32)
        inv = tail[:, ROPE : ROPE + 1] + tail[:, ROPE + 1 : ROPE + 2]
        sums_ref[pl.ds(block, 1), :] = jnp.sum(grad, axis=0, keepdims=True)
        weighted_ref[pl.ds(block, 1), :] = jnp.sum(grad * inv, axis=0, keepdims=True)
        products = grad * proj_ref[span(block), :]
        narrow = products[:, :128]
        for start in range(128, products.shape[1], 128):
            narrow = narrow + products[:, start : start + 128]
        row_ref[pl.ds(block, 1), :] = jnp.sum(narrow.T, axis=0, keepdims=True)

    each_block(reduce)
    weighted = weighted_ref[...]
    high = weighted.astype(bf16)
    low = (weighted - high.astype(f32)).astype(bf16)
    both = contract_last(jnp.concatenate([high, low], axis=0), weight_ref[...])
    back = both[:nblocks] + both[nblocks:]
    out_ref[...] = jnp.zeros_like(out_ref)
    chunks = []
    for array in (back, row_ref[...], sums_ref[...]):
        for start in range(0, array.shape[1], 128):
            chunks.append(array[:, start : start + 128])
    for index, chunk in enumerate(chunks):
        for block in range(nblocks):
            out_ref[block, index : index + 1, :] = chunk[block : block + 1, :]


def full(shape):
    return pl.BlockSpec(shape, lambda *unused: (0,) * len(shape))


def params():
    return pltpu.CompilerParams(vmem_limit_bytes=VMEM_LIMIT)


def cost(flops, moved):
    return pl.CostEstimate(flops=flops, bytes_accessed=moved, transcendentals=0)


def spread(
    ring, head_shards, q_latent, latent_bias, norm_gain, w_q, steer, kv_latent, key_rope, w_uk, w_uv, d_out, block_mask
):
    ql = q_latent.shape[1]
    queries = ring * BLK
    mine = lax.axis_index("ctx")
    lane = lax.axis_index("head")
    columns = w_q.shape[1] // ring
    cot_columns = d_out.shape[1] // ring
    heads = cot_columns // VD
    shifts = range(1, ring)

    def chunk(array, width, step):
        return lax.dynamic_slice_in_dim(array, (mine + step) % ring * width, width, 1)

    def send(array, axis, target, size):
        return lax.ppermute(array, axis, [(i, target(i)) for i in range(size)])

    def turn(array, step):
        return send(array, "ctx", lambda i: (i + step) % ring, ring)

    gain_row = norm_gain[None, :]
    payload_width = ql + KVL + 2 * ROPE
    piece = pl.pallas_call(
        prep_kernel,
        out_shape=jax.ShapeDtypeStruct((PIECE, payload_width), bf16),
        grid_spec=pltpu.PrefetchScalarGridSpec(
            num_scalar_prefetch=1,
            grid=(1,),
            in_specs=[
                pl.BlockSpec((PIECE, ql), lambda i, pick: (pick[0], 0)),
                full((1, ql)),
                full((1, ql)),
                pl.BlockSpec((PIECE, KVL), lambda i, pick: (pick[0], 0)),
                pl.BlockSpec((PIECE, ROPE), lambda i, pick: (pick[0], 0)),
            ],
            out_specs=full((PIECE, payload_width)),
        ),
        cost_estimate=cost(10**6, 10**6),
    )(lane[None], q_latent, latent_bias, gain_row, kv_latent, key_rope)
    pieces = [piece] + [turn(piece, 2 * step) for step in range(1, ring // 2)]
    weight_parts = [chunk(w_q, columns, 0)] + [turn(chunk(w_q, columns, step), step) for step in shifts]
    first = jnp.stack(pieces)
    second = send(first, "ctx", lambda i: i ^ 1, ring)
    both = jnp.concatenate([first, second])
    other = send(both, "head", lambda i: i ^ 2, head_shards)
    near = jnp.concatenate([both, other])
    far = send(near, "head", lambda i: i ^ 1, head_shards)
    cot_parts = [chunk(d_out, cot_columns, 0)] + [turn(chunk(d_out, cot_columns, step), step) for step in shifts]
    all_steer = lax.all_to_all(steer.reshape(ring, columns), "ctx", 0, 0, tiled=True)

    z, x = mine // 2, mine % 2
    places = []
    for core in range(2):
        for y in range(2):
            for dx in range(2):
                for step in range(ring // 2):
                    block = (z + ring // 2 - step) % (ring // 2) * 2 + (x + dx) % 2
                    places.append(block * BLK + PIECE * (lane ^ (2 * y + core)))
    places = jnp.stack(places).astype(jnp.int32)
    sources = jnp.stack([(mine + ring - step) % ring for step in range(ring)]).astype(jnp.int32)

    c_query, tail, wide, values = pl.pallas_call(
        keys_kernel,
        out_shape=(
            jax.ShapeDtypeStruct((queries, ql), bf16),
            jax.ShapeDtypeStruct((queries, 2 * ROPE), bf16),
            jax.ShapeDtypeStruct((heads, queries, WIDE), bf16),
            jax.ShapeDtypeStruct((queries, heads * VD), bf16),
        ),
        grid_spec=pltpu.PrefetchScalarGridSpec(
            num_scalar_prefetch=1,
            grid=(1,),
            in_specs=[
                full((16, PIECE, payload_width)),
                full((16, PIECE, payload_width)),
                pl.BlockSpec((KVL, heads * NOPE), lambda i, place: (0, place[32])),
                pl.BlockSpec((KVL, heads * VD), lambda i, place: (0, place[32])),
            ],
            out_specs=(
                full((queries, ql)),
                full((queries, 2 * ROPE)),
                full((heads, queries, WIDE)),
                full((queries, heads * VD)),
            ),
            scratch_shapes=[pltpu.VMEM((queries, KVL), bf16)],
        ),
        compiler_params=params(),
        cost_estimate=cost(2 * 10**9, 10**7),
    )(jnp.concatenate([places, mine[None]]), near, far, w_uk, w_uv)

    query, projected, weight = pl.pallas_call(
        query_kernel,
        out_shape=(
            jax.ShapeDtypeStruct((queries, columns), bf16),
            jax.ShapeDtypeStruct((queries, columns), f32),
            jax.ShapeDtypeStruct((ql, columns), bf16),
        ),
        grid_spec=pltpu.PrefetchScalarGridSpec(
            num_scalar_prefetch=1,
            grid=(1,),
            in_specs=[full(weight_parts[0].shape)] * ring + [full((queries, ql)), full((ring, columns))],
            out_specs=(full((queries, columns)), full((queries, columns)), full((ql, columns))),
        ),
        compiler_params=params(),
        cost_estimate=cost(3 * 10**9, 10**7),
    )(sources, *weight_parts, c_query, all_steer)

    used = (ql + BLK + columns) // 128
    slots = (used + 7) // 8 * 8
    pairs = (ring * ring + UNROLL - 1) // UNROLL * UNROLL
    sums = pl.pallas_call(
        attend_kernel,
        out_shape=jax.ShapeDtypeStruct((ring, slots, 128), f32),
        grid_spec=pltpu.PrefetchScalarGridSpec(
            num_scalar_prefetch=2,
            grid=(1,),
            in_specs=[full((BLK, cot_columns))] * ring
            + [
                full((queries, columns)),
                full((queries, columns)),
                full((queries, 2 * ROPE)),
                full((heads, queries, WIDE)),
                full((queries, heads * VD)),
                full((ql, columns)),
            ],
            out_specs=full((ring, slots, 128)),
            scratch_shapes=[
                pltpu.VMEM((ring, BLK, cot_columns), bf16),
                pltpu.VMEM((ring, columns), f32),
                pltpu.VMEM((ring, columns), f32),
                pltpu.VMEM((ring, BLK), f32),
                pltpu.VMEM((pairs, heads, BLK, BLK), f32),
                pltpu.VMEM((pairs, heads, BLK, BLK), f32),
                pltpu.VMEM((ring + 1, heads, BLK, BLK), f32),
                pltpu.VMEM((ring + 1, heads, BLK, BLK), f32),
                pltpu.VMEM((ring + 1, BLK, columns), f32),
                pltpu.SMEM((2, pairs + UNROLL), jnp.int32),
            ],
        ),
        compiler_params=params(),
        cost_estimate=cost(8 * 10**9, 10**7),
    )(block_mask, sources, *cot_parts, query, projected, tail, wide, values, weight)

    arrived = lax.all_to_all(sums, "ctx", 0, 0, tiled=True)
    cut = (ql + BLK) // 128
    grad_steer = arrived[:, cut:used].reshape(1, ring * columns)
    local = jnp.sum(arrived[:, :cut], axis=0)
    summed = local
    for bits in range(1, head_shards):
        summed = summed + lax.ppermute(local, "head", [(i, i ^ bits) for i in range(head_shards)])
    back = summed[: ql // 128].reshape(1, ql)
    dots = summed[ql // 128 : cut].reshape(BLK, 1)
    shifted = q_latent.astype(f32) + latent_bias
    inv = lax.rsqrt(jnp.mean(shifted * shifted, axis=1, keepdims=True) + epsilon)
    pull = jnp.sum(shifted * (inv * inv * dots / ql), axis=0, keepdims=True)
    return (grad_steer, back * gain_row - pull)


def solution(mesh):
    ring, head_shards = mesh.shape["ctx"], mesh.shape["head"]

    def body(*arrays):
        heads = arrays[7].shape[1] // NOPE
        fits = arrays[0].shape[0] == BLK and ring == 8 and head_shards == 4 and heads % (2 * ring) == 0
        if fits:
            return spread(ring, head_shards, *arrays)
        return shards(*arrays)

    in_specs = (
        P("ctx", None),
        P("ctx", None),
        P(),
        P("ctx", "head"),
        P("ctx", "head"),
        P("ctx", None),
        P("ctx", None),
        P(None, "head"),
        P(None, "head"),
        P("ctx", "head"),
        P(),
    )
    out_specs = (P("ctx", "head"), P("ctx", None))
    return jax.shard_map(body, mesh=mesh, in_specs=in_specs, out_specs=out_specs, check_vma=False)
```

```python
import math

import jax
import jax.numpy as jnp
from jax import lax
from jax.experimental import pallas as pl
from jax.experimental.pallas import tpu as pltpu
from jax.sharding import PartitionSpec as P

KVL = 512
NOPE = 128
ROPE = 64
VD = 128
BLK = 128


epsilon = 1e-06
lowest = -1e30


def contract_last(left, right):
    return lax.dot_general(
        left, right, (((1,), (1,)), ((), ())), preferred_element_type=jnp.float32
    )


def shards(
    q_latent, latent_bias, norm_gain, w_q, steer, kv_latent, key_rope, w_uk, w_uv, d_out, block_mask
):
    queries = q_latent.shape[0]
    nblocks = queries // BLK
    head_count = w_uk.shape[1] // NOPE
    head_width = NOPE + ROPE
    score_scale = head_width ** (-0.5)
    row_count = queries * head_count
    shifted = q_latent.astype(jnp.float32) + jnp.repeat(latent_bias, BLK, axis=0)
    inv_rms = lax.rsqrt(jnp.mean(shifted * shifted, axis=1, keepdims=True) + epsilon)
    normed = shifted * inv_rms
    c_query = (normed * norm_gain).astype(jnp.bfloat16)
    full_wq = lax.all_gather(w_q, "ctx", axis=0, tiled=True)
    projected = jnp.dot(c_query, full_wq, preferred_element_type=jnp.float32)
    query_all = (
        (projected + jnp.repeat(steer, BLK, axis=0))
        .astype(jnp.bfloat16)
        .reshape(queries, head_count, head_width)
    )
    q_rope = query_all[:, :, NOPE:].reshape(row_count, ROPE)
    key_up = w_uk.reshape(KVL, head_count, NOPE)
    value_up = w_uv.reshape(KVL, head_count, VD)
    q_absorbed = (
        jnp.einsum(
            "qhn,khn->qhk", query_all[:, :, :NOPE], key_up, preferred_element_type=jnp.float32
        )
        .astype(jnp.bfloat16)
        .reshape(row_count, KVL)
    )
    g_absorbed = (
        jnp.einsum(
            "qhv,khv->qhk",
            d_out.reshape(queries, head_count, VD),
            value_up,
            preferred_element_type=jnp.float32,
        )
        .astype(jnp.bfloat16)
        .reshape(row_count, KVL)
    )
    my_mask = lax.dynamic_slice_in_dim(block_mask, lax.axis_index("ctx") * nblocks, nblocks, 0)
    start_status = (
        jnp.full((row_count,), lowest, jnp.float32),
        jnp.zeros((row_count,), jnp.float32),
        jnp.zeros((row_count,), jnp.float32),
        jnp.zeros((2 * row_count, KVL), jnp.float32),
        jnp.zeros((2 * row_count, ROPE), jnp.float32),
    )
    lat_portion = lax.all_gather(kv_latent, "ctx", axis=0, tiled=True)
    rope_portion = lax.all_gather(key_rope, "ctx", axis=0, tiled=True)
    key_total = lat_portion.shape[0]
    tile_len = math.gcd(key_total, BLK)
    tile_count = key_total // tile_len

    def visit_tile(status, inputs):
        lat_tile, rope_tile, offset = inputs
        key_block = offset * tile_len // BLK
        column = lax.dynamic_index_in_dim(my_mask, key_block, 1, keepdims=False)

        def update(status):
            peak, total_weight, weighted, lat_acc, rope_acc = status
            live_rows = jnp.repeat(column > 0, head_count * BLK)[:, None]
            scores = (
                contract_last(q_absorbed, lat_tile) + contract_last(q_rope, rope_tile)
            ) * score_scale
            scores = jnp.where(live_rows, scores, lowest)
            new_peak = jnp.maximum(peak, jnp.max(scores, axis=1))
            factor = jnp.exp(peak - new_peak)
            weights = jnp.where(live_rows, jnp.exp(scores - new_peak[:, None]), 0.0)
            dots = contract_last(g_absorbed, lat_tile)
            mixed = weights * dots
            total_weight = total_weight * factor + jnp.sum(weights, axis=1)
            weighted = weighted * factor + jnp.sum(mixed, axis=1)
            stacked = jnp.concatenate([mixed, weights], axis=0).astype(jnp.bfloat16)
            doubled = jnp.concatenate([factor, factor])[:, None]
            lat_acc = lat_acc * doubled + jnp.dot(
                stacked, lat_tile, preferred_element_type=jnp.float32
            )
            rope_acc = rope_acc * doubled + jnp.dot(
                stacked, rope_tile, preferred_element_type=jnp.float32
            )
            return (new_peak, total_weight, weighted, lat_acc, rope_acc)

        def keep_status(status):
            return status

        return (lax.cond(jnp.max(column) > 0, update, keep_status, status), None)

    offsets = jnp.arange(tile_count, dtype=jnp.int32)
    tiles = (
        lat_portion.reshape(tile_count, tile_len, KVL),
        rope_portion.reshape(tile_count, tile_len, ROPE),
        offsets,
    )
    result, _ = lax.scan(visit_tile, start_status, tiles)
    _, total_weight, weighted, lat_acc, rope_acc = result
    ratio = (weighted / total_weight)[:, None]
    inverse = (score_scale / total_weight)[:, None]
    grad_lat = ((lat_acc[:row_count] - ratio * lat_acc[row_count:]) * inverse).astype(jnp.bfloat16)
    grad_rope = (rope_acc[:row_count] - ratio * rope_acc[row_count:]) * inverse
    grad_nope = jnp.einsum(
        "qhk,khn->qhn",
        grad_lat.reshape(queries, head_count, KVL),
        key_up,
        preferred_element_type=jnp.float32,
    )
    grad_query = jnp.concatenate(
        [grad_nope, grad_rope.reshape(queries, head_count, ROPE)], axis=2
    ).reshape(queries, head_count * head_width)
    grad_steer = jnp.sum(grad_query.reshape(nblocks, BLK, head_count * head_width), axis=1)
    grad_round = grad_query.astype(jnp.bfloat16)
    partial_grad = contract_last(grad_round, full_wq)
    latent_grad = lax.psum(partial_grad.astype(jnp.bfloat16), "head").astype(jnp.float32)
    scaled = latent_grad * norm_gain
    project_mean = jnp.mean(scaled * normed, axis=1, keepdims=True)
    grad_shifted = inv_rms * (scaled - normed * project_mean)
    grad_bias = jnp.sum(grad_shifted.reshape(nblocks, BLK, grad_shifted.shape[1]), axis=1)
    return (grad_steer, grad_bias)


WIDE = 256
PIECE = 32
UNROLL = 2
VMEM_LIMIT = 60 * 1024 * 1024
f32 = jnp.float32
bf16 = jnp.bfloat16


def dot(left, right):
    return jnp.dot(left, right, preferred_element_type=f32)


def prep_kernel(pick, lat_ref, bias_ref, gain_ref, kv_ref, rope_ref, out_ref):
    ql = lat_ref.shape[1]
    shifted = lat_ref[...].astype(f32) + bias_ref[...]
    inv = lax.rsqrt(jnp.mean(shifted * shifted, axis=1, keepdims=True) + epsilon)
    out_ref[:, :ql] = (shifted * inv * gain_ref[...]).astype(bf16)
    out_ref[:, ql : ql + KVL] = kv_ref[...]
    out_ref[:, ql + KVL : ql + KVL + ROPE] = rope_ref[...]
    high = inv.astype(bf16)
    low = (inv - high.astype(f32)).astype(bf16)
    lane = lax.broadcasted_iota(jnp.int32, (lat_ref.shape[0], ROPE), 1)
    pair = jnp.where(lane == 0, high.astype(f32), jnp.where(lane == 1, low.astype(f32), 0.0))
    out_ref[:, ql + KVL + ROPE :] = pair.astype(bf16)


def keys_kernel(place, near_ref, far_ref, uk_ref, uv_ref, c_ref, tail_ref, wide_ref, value_ref, kv_ref):
    ql = c_ref.shape[1]
    for position, ref in ((0, near_ref), (1, far_ref)):
        for piece in range(16):
            rows = pl.ds(pl.multiple_of(place[position * 16 + piece], PIECE), PIECE)
            c_ref[rows, :] = ref[piece, :, :ql]
            kv_ref[rows, :] = ref[piece, :, ql : ql + KVL]
            tail_ref[rows, :] = ref[piece, :, ql + KVL :]
    heads = wide_ref.shape[0]
    step = 256
    lane = lax.broadcasted_iota(jnp.int32, (step, NOPE), 1)
    for start in range(0, c_ref.shape[0], step):
        rows = slice(start, start + step)
        kv = kv_ref[rows, :]
        up = dot(kv, uk_ref[...])
        value_ref[rows, :] = dot(kv, uv_ref[...]).astype(bf16)
        rope = jnp.where(lane < ROPE, tail_ref[rows, :].astype(f32), 0.0)
        for head in range(heads):
            full = jnp.concatenate([up[:, head * NOPE : (head + 1) * NOPE], rope], axis=1)
            if head % 2:
                full = pltpu.roll(full, ROPE, 1)
            wide_ref[head, rows, :] = full.astype(bf16)


def query_kernel(place, *refs):
    count = (len(refs) - 5) // 2
    weights, steers = refs[:count], refs[count : 2 * count]
    c_ref, q_ref, proj_ref, full_ref, steer_ref = refs[2 * count :]
    depth = weights[0].shape[0]
    for index in range(count):
        full_ref[pl.ds(pl.multiple_of(place[index] * depth, 64), depth), :] = weights[index][...]
        steer_ref[pl.ds(place[index], 1), :] = steers[index][...]
    step = 256
    for start in range(0, c_ref.shape[0], step):
        projected = dot(c_ref[start : start + step, :], full_ref[...])
        proj_ref[start : start + step, :] = projected
        for part in range(step // BLK):
            block = start // BLK + part
            low = part * BLK
            q_ref[start + low : start + low + BLK, :] = (
                projected[low : low + BLK] + steer_ref[block : block + 1, :]
            ).astype(bf16)


def list_pairs(mask, pair_ref, nblocks):
    def list_step(index, found):
        block, key = index // mask.shape[1], index % mask.shape[1]
        pair_ref[0, found] = block
        pair_ref[1, found] = key
        return found + (mask[block, key] > 0).astype(jnp.int32)

    found = lax.fori_loop(0, nblocks * mask.shape[1], list_step, 0)
    pair_ref[0, found] = nblocks
    pair_ref[1, found] = 0
    return found


def each_pair(found, pair_ref, visit):
    def trip(index, carry):
        for part in range(UNROLL):
            pair = index * UNROLL + part
            visit(pair, pair_ref[0, pair], pair_ref[1, pair])
        return carry

    lax.fori_loop(0, (found + UNROLL - 1) // UNROLL, trip, 0)


def each(count, visit):
    def trip(index, carry):
        visit(index)
        return carry

    lax.fori_loop(0, count, trip, 0)


def span(block):
    return pl.ds(pl.multiple_of(block * BLK, BLK), BLK)


def window(head):
    left = head // 2 * 2 * (NOPE + ROPE) + head % 2 * NOPE
    return slice(left, left + WIDE)


def weights_kernel(mask, q_ref, wide_ref, out_ref, score_ref, sum_ref, peak_ref, pair_ref, sems):
    nblocks = mask.shape[0]
    heads = wide_ref.shape[0]
    scale = (NOPE + ROPE) ** (-0.5)
    found = list_pairs(mask, pair_ref, nblocks)
    sum_ref[...] = jnp.full_like(sum_ref, lowest)

    def score(pair, block, key):
        rows = span(jnp.minimum(block, nblocks - 1))
        for head in range(heads):
            scores = contract_last(q_ref[rows, window(head)], wide_ref[head, span(key), :]) * scale
            score_ref[pair, head] = scores
            sum_ref[block, head] = jnp.maximum(sum_ref[block, head], scores)

    each_pair(found, pair_ref, score)

    def find_peak(block):
        for head in range(heads):
            peak = jnp.max(sum_ref[block, head], axis=1, keepdims=True)
            peak_ref[block, head] = jnp.broadcast_to(peak, (BLK, BLK))
            sum_ref[block, head] = jnp.zeros((BLK, BLK), f32)

    each(nblocks + 1, find_peak)

    def weigh(pair, block, key):
        for head in range(heads):
            weights = jnp.exp(score_ref[pair, head] - peak_ref[block, head])
            score_ref[pair, head] = weights
            sum_ref[block, head] = sum_ref[block, head] + weights

    each_pair(found, pair_ref, weigh)

    def invert(block):
        for head in range(heads):
            total = jnp.sum(sum_ref[block, head], axis=1, keepdims=True)
            peak_ref[block, head] = jnp.broadcast_to(1.0 / total, (BLK, BLK))

    each(nblocks, invert)

    def copy(pair):
        return pltpu.make_async_copy(score_ref.at[pair], out_ref.at[pair], sems.at[pair])

    def finish(pair):
        block = pair_ref[0, pair]
        for head in range(heads):
            score_ref[pair, head] = score_ref[pair, head] * peak_ref[block, head]
        copy(pair).start()

    each(found, finish)
    each(found, lambda pair: copy(pair).wait())


def slope_kernel(mask, place, *refs):
    count = len(refs) - 17
    cots = refs[:count]
    (
        held_ref, proj_ref, tail_ref, wide_ref, value_ref, weight_ref, out_ref,
        cot_ref, sums_ref, weighted_ref, row_ref, prob_ref, dot_ref, mean_ref, grad_ref, pair_ref, sems,
    ) = refs[count:]
    nblocks = count
    heads = wide_ref.shape[0]
    scale = (NOPE + ROPE) ** (-0.5)
    found = list_pairs(mask, pair_ref, nblocks)

    def copy(pair):
        return pltpu.make_async_copy(held_ref.at[pair], prob_ref.at[pair], sems.at[pair])

    each(found, lambda pair: copy(pair).start())
    for index, ref in enumerate(cots):
        cot_ref[place[index]] = ref[...]
    mean_ref[...] = jnp.zeros_like(mean_ref)
    grad_ref[...] = jnp.zeros_like(grad_ref)
    each(found, lambda pair: copy(pair).wait())

    def weigh(pair, block, key):
        source = jnp.minimum(block, nblocks - 1)
        for head in range(heads):
            lanes = slice(head * VD, (head + 1) * VD)
            dots = contract_last(cot_ref[source, :, lanes], value_ref[span(key), lanes])
            dot_ref[pair, head] = dots
            mean_ref[block, head] = mean_ref[block, head] + prob_ref[pair, head] * dots

    each_pair(found, pair_ref, weigh)

    def average(block):
        for head in range(heads):
            mean = jnp.sum(mean_ref[block, head], axis=1, keepdims=True)
            mean_ref[block, head] = jnp.broadcast_to(mean, (BLK, BLK))

    each(nblocks, average)

    def gather(pair, block, key):
        for head in range(heads):
            slope = prob_ref[pair, head] * (dot_ref[pair, head] - mean_ref[block, head])
            gained = dot(slope.astype(bf16), wide_ref[head, span(key), :])
            grad_ref[block, :, window(head)] = grad_ref[block, :, window(head)] + gained

    each_pair(found, pair_ref, gather)

    def reduce(block):
        grad = grad_ref[block] * scale
        tail = tail_ref[span(block), :].astype(f32)
        inv = tail[:, ROPE : ROPE + 1] + tail[:, ROPE + 1 : ROPE + 2]
        sums_ref[pl.ds(block, 1), :] = jnp.sum(grad, axis=0, keepdims=True)
        weighted_ref[pl.ds(block, 1), :] = jnp.sum(grad * inv, axis=0, keepdims=True)
        products = grad * proj_ref[span(block), :]
        narrow = products[:, :128]
        for start in range(128, products.shape[1], 128):
            narrow = narrow + products[:, start : start + 128]
        row_ref[pl.ds(block, 1), :] = jnp.sum(narrow.T, axis=0, keepdims=True)

    each(nblocks, reduce)
    weighted = weighted_ref[...]
    high = weighted.astype(bf16)
    low = (weighted - high.astype(f32)).astype(bf16)
    both = contract_last(jnp.concatenate([high, low], axis=0), weight_ref[...])
    back = both[:nblocks] + both[nblocks:]
    out_ref[...] = jnp.zeros_like(out_ref)
    chunks = []
    for array in (back, row_ref[...], sums_ref[...]):
        for start in range(0, array.shape[1], 128):
            chunks.append(array[:, start : start + 128])
    for index, chunk in enumerate(chunks):
        for block in range(nblocks):
            out_ref[block, index : index + 1, :] = chunk[block : block + 1, :]


def full(shape):
    return pl.BlockSpec(shape, lambda *unused: (0,) * len(shape))


def params():
    return pltpu.CompilerParams(vmem_limit_bytes=VMEM_LIMIT)


def cost(flops, moved):
    return pl.CostEstimate(flops=flops, bytes_accessed=moved, transcendentals=0)


def spread(
    ring, head_shards, q_latent, latent_bias, norm_gain, w_q, steer, kv_latent, key_rope, w_uk, w_uv, d_out, block_mask
):
    ql = q_latent.shape[1]
    queries = ring * BLK
    mine = lax.axis_index("ctx")
    lane = lax.axis_index("head")
    columns = w_q.shape[1] // ring
    cot_columns = d_out.shape[1] // ring
    heads = cot_columns // VD
    shifts = range(1, ring)

    def chunk(array, width, step):
        return lax.dynamic_slice_in_dim(array, (mine + step) % ring * width, width, 1)

    def send(array, axis, target, size):
        return lax.ppermute(array, axis, [(i, target(i)) for i in range(size)])

    def turn(array, step):
        return send(array, "ctx", lambda i: (i + step) % ring, ring)

    gain_row = norm_gain[None, :]
    payload_width = ql + KVL + 2 * ROPE
    piece = pl.pallas_call(
        prep_kernel,
        out_shape=jax.ShapeDtypeStruct((PIECE, payload_width), bf16),
        grid_spec=pltpu.PrefetchScalarGridSpec(
            num_scalar_prefetch=1,
            grid=(1,),
            in_specs=[
                pl.BlockSpec((PIECE, ql), lambda i, pick: (pick[0], 0)),
                full((1, ql)),
                full((1, ql)),
                pl.BlockSpec((PIECE, KVL), lambda i, pick: (pick[0], 0)),
                pl.BlockSpec((PIECE, ROPE), lambda i, pick: (pick[0], 0)),
            ],
            out_specs=full((PIECE, payload_width)),
        ),
        cost_estimate=cost(10**6, 10**6),
    )(lane[None], q_latent, latent_bias, gain_row, kv_latent, key_rope)
    pieces = [piece] + [turn(piece, 2 * step) for step in range(1, ring // 2)]
    weight_parts = [chunk(w_q, columns, 0)] + [turn(chunk(w_q, columns, step), step) for step in shifts]
    first = jnp.stack(pieces)
    second = send(first, "ctx", lambda i: i ^ 1, ring)
    both = jnp.concatenate([first, second])
    other = send(both, "head", lambda i: i ^ 2, head_shards)
    near = jnp.concatenate([both, other])
    far = send(near, "head", lambda i: i ^ 1, head_shards)
    cot_parts = [chunk(d_out, cot_columns, 0)] + [turn(chunk(d_out, cot_columns, step), step) for step in shifts]
    steer_parts = [chunk(steer, columns, 0)] + [turn(chunk(steer, columns, step), step) for step in shifts]

    z, x = mine // 2, mine % 2
    places = []
    for core in range(2):
        for y in range(2):
            for dx in range(2):
                for step in range(ring // 2):
                    block = (z + ring // 2 - step) % (ring // 2) * 2 + (x + dx) % 2
                    places.append(block * BLK + PIECE * (lane ^ (2 * y + core)))
    places = jnp.stack(places).astype(jnp.int32)
    sources = jnp.stack([(mine + ring - step) % ring for step in range(ring)]).astype(jnp.int32)

    c_query, tail, wide, values = pl.pallas_call(
        keys_kernel,
        out_shape=(
            jax.ShapeDtypeStruct((queries, ql), bf16),
            jax.ShapeDtypeStruct((queries, 2 * ROPE), bf16),
            jax.ShapeDtypeStruct((heads, queries, WIDE), bf16),
            jax.ShapeDtypeStruct((queries, heads * VD), bf16),
        ),
        grid_spec=pltpu.PrefetchScalarGridSpec(
            num_scalar_prefetch=1,
            grid=(1,),
            in_specs=[
                full((16, PIECE, payload_width)),
                full((16, PIECE, payload_width)),
                pl.BlockSpec((KVL, heads * NOPE), lambda i, place: (0, place[32])),
                pl.BlockSpec((KVL, heads * VD), lambda i, place: (0, place[32])),
            ],
            out_specs=(
                full((queries, ql)),
                full((queries, 2 * ROPE)),
                full((heads, queries, WIDE)),
                full((queries, heads * VD)),
            ),
            scratch_shapes=[pltpu.VMEM((queries, KVL), bf16)],
        ),
        compiler_params=params(),
        cost_estimate=cost(2 * 10**9, 10**7),
    )(jnp.concatenate([places, mine[None]]), near, far, w_uk, w_uv)

    query, projected, weight = pl.pallas_call(
        query_kernel,
        out_shape=(
            jax.ShapeDtypeStruct((queries, columns), bf16),
            jax.ShapeDtypeStruct((queries, columns), f32),
            jax.ShapeDtypeStruct((ql, columns), bf16),
        ),
        grid_spec=pltpu.PrefetchScalarGridSpec(
            num_scalar_prefetch=1,
            grid=(1,),
            in_specs=[full(weight_parts[0].shape)] * ring + [full((1, columns))] * ring + [full((queries, ql))],
            out_specs=(full((queries, columns)), full((queries, columns)), full((ql, columns))),
            scratch_shapes=[pltpu.VMEM((ring, columns), f32)],
        ),
        compiler_params=params(),
        cost_estimate=cost(3 * 10**9, 10**7),
    )(sources, *weight_parts, *steer_parts, c_query)

    used = (ql + BLK + columns) // 128
    slots = (used + 7) // 8 * 8
    pairs = (ring * ring + UNROLL - 1) // UNROLL * UNROLL
    tiles = (pairs, heads, BLK, BLK)
    held = pl.pallas_call(
        weights_kernel,
        out_shape=jax.ShapeDtypeStruct(tiles, f32),
        grid_spec=pltpu.PrefetchScalarGridSpec(
            num_scalar_prefetch=1,
            grid=(1,),
            in_specs=[full((queries, columns)), full((heads, queries, WIDE))],
            out_specs=pl.BlockSpec(memory_space=pl.ANY),
            scratch_shapes=[
                pltpu.VMEM(tiles, f32),
                pltpu.VMEM((ring + 1, heads, BLK, BLK), f32),
                pltpu.VMEM((ring + 1, heads, BLK, BLK), f32),
                pltpu.SMEM((2, pairs + UNROLL), jnp.int32),
                pltpu.SemaphoreType.DMA((pairs,)),
            ],
        ),
        compiler_params=params(),
        cost_estimate=cost(2 * 10**9, 10**7),
    )(block_mask, query, wide)
    sums = pl.pallas_call(
        slope_kernel,
        out_shape=jax.ShapeDtypeStruct((ring, slots, 128), f32),
        grid_spec=pltpu.PrefetchScalarGridSpec(
            num_scalar_prefetch=2,
            grid=(1,),
            in_specs=[full((BLK, cot_columns))] * ring
            + [
                pl.BlockSpec(memory_space=pl.ANY),
                full((queries, columns)),
                full((queries, 2 * ROPE)),
                full((heads, queries, WIDE)),
                full((queries, heads * VD)),
                full((ql, columns)),
            ],
            out_specs=full((ring, slots, 128)),
            scratch_shapes=[
                pltpu.VMEM((ring, BLK, cot_columns), bf16),
                pltpu.VMEM((ring, columns), f32),
                pltpu.VMEM((ring, columns), f32),
                pltpu.VMEM((ring, BLK), f32),
                pltpu.VMEM(tiles, f32),
                pltpu.VMEM(tiles, f32),
                pltpu.VMEM((ring + 1, heads, BLK, BLK), f32),
                pltpu.VMEM((ring + 1, BLK, columns), f32),
                pltpu.SMEM((2, pairs + UNROLL), jnp.int32),
                pltpu.SemaphoreType.DMA((pairs,)),
            ],
        ),
        compiler_params=params(),
        cost_estimate=cost(4 * 10**9, 10**7),
    )(block_mask, sources, *cot_parts, held, projected, tail, wide, values, weight)

    arrived = lax.all_to_all(sums, "ctx", 0, 0, tiled=True)
    cut = (ql + BLK) // 128
    grad_steer = arrived[:, cut:used].reshape(1, ring * columns)
    local = jnp.sum(arrived[:, :cut], axis=0)
    summed = local
    for bits in range(1, head_shards):
        summed = summed + lax.ppermute(local, "head", [(i, i ^ bits) for i in range(head_shards)])
    back = summed[: ql // 128].reshape(1, ql)
    dots = summed[ql // 128 : cut].reshape(BLK, 1)
    shifted = q_latent.astype(f32) + latent_bias
    inv = lax.rsqrt(jnp.mean(shifted * shifted, axis=1, keepdims=True) + epsilon)
    pull = jnp.sum(shifted * (inv * inv * dots / ql), axis=0, keepdims=True)
    return (grad_steer, back * gain_row - pull)


def solution(mesh):
    ring, head_shards = mesh.shape["ctx"], mesh.shape["head"]

    def body(*arrays):
        heads = arrays[7].shape[1] // NOPE
        fits = arrays[0].shape[0] == BLK and ring == 8 and head_shards == 4 and heads % (2 * ring) == 0
        if fits:
            return spread(ring, head_shards, *arrays)
        return shards(*arrays)

    in_specs = (
        P("ctx", None),
        P("ctx", None),
        P(),
        P("ctx", "head"),
        P("ctx", "head"),
        P("ctx", None),
        P("ctx", None),
        P(None, "head"),
        P(None, "head"),
        P("ctx", "head"),
        P(),
    )
    out_specs = (P("ctx", "head"), P("ctx", None))
    return jax.shard_map(body, mesh=mesh, in_specs=in_specs, out_specs=out_specs, check_vma=False)
```
